128 devices in a mesh: blk: 64 (over y, x, z_lo, core), dim: 2 (over z_hi).
Axes of the slice: x: 4, y: 4, z: 4 (z_hi: 2, z_lo: 2; z = z_hi * 2 + z_lo), core: 2. Of those that a mesh axis runs over, the one named last changes fastest.
Arguments:
- points: bfloat16 [65536, 1024], P('blk', 'dim'), may hold values from -6 to 6
- owner: int32 [65536, 1], P('blk'), may hold values from 0 to 63; in each aligned block of 1024 rows (0 to 1023, 1024 to 2047, ...) at most 32 rows name the same one
- member: int32 [65536], P('blk'), may hold values from 0 to 8191
- centroids: bfloat16 [524288, 1024], P('blk', 'dim'), may hold values from -3 to 3
Outputs:
- new_centroids: bfloat16 [524288, 1024], P('blk', 'dim')
- nearest: float32 [65536], P('blk')
The draws below stay inside these ranges and needn't reach their ends.
Inputs may be any that keep to these rules, and one draw needn't show every extreme that they name: In the rows of one index of blk, no owner value occurs more than 32 times, and some value occurs exactly 32 times.
All inputs are finite; a program needn't handle non-finite values.
Results may differ from the reference program's by a relative error of at most 0.0004.
Values may be sent and summed in bfloat16 or wider, within the bound.
No kernel may reach another device: no remote copies, remote signals or barrier semaphores. Data moves between devices by JAX's collectives and lax.ppermute only.
A program may use at most 128 MiB of HBM per device.

```python
import math
import jax
import jax.numpy as jnp
import numpy as np
from jax import lax

D = 1024
KC_DEV = 8192
PTS_DEV = 1024
CYCLE = 2
LISTS = 524288
POINTS = 65536
N_BLK = 64


def set_ends(array, stream_key, low, top_value):
    spot = [jax.random.randint(jax.random.fold_in(stream_key, axis), (), 0, length) for axis, length in enumerate(array.shape)]
    main_axis = array.shape.index(max(array.shape))
    neighbour = spot[:main_axis] + [(spot[main_axis] + 1) % array.shape[main_axis]] + spot[main_axis + 1:]
    return array.at[tuple(spot)].set(low).at[tuple(neighbour)].set(top_value)


def level_of(key, dims, shards, low, high):
    loudness = 1.0
    for position, parts in shards:
        heights = jax.random.uniform(jax.random.fold_in(jax.random.fold_in(key, 6), position), (parts,), jnp.float32, low / len(shards), high / len(shards))
        loudness = loudness * jnp.repeat(jnp.exp(heights), dims[position] // parts).reshape((-1,) + (1,) * (len(dims) - 1 - position))
    return loudness


def shared_out(stream_key, own, number, rows, amount, top, bound, lean):
    order = jax.random.permutation(stream_key, amount)
    packed, common = shares(amount, rows * top, bound, lean, True), shares(amount, rows * top, bound, lean, False)
    places = jnp.arange(amount)

    def named(sizes, rotation):
        used = int((sizes > 0).sum())
        fixed = max(1, used // 4)
        passed = fixed + (places - fixed + rotation * (used - fixed)) % max(1, amount - fixed)
        return jnp.zeros((amount,), jnp.int32).at[order[jnp.where(places < fixed, places, passed)]].set(jnp.asarray(sizes, jnp.int32))

    sizes = jnp.where(number % 4 == 0, named(packed, number // 4), named(common, number - number // 4 - 1))
    mixed = jax.random.permutation(jax.random.fold_in(own, 3), amount)
    giver, receiver = mixed[0:amount // 2 * 2:2], mixed[1:amount // 2 * 2:2]
    slack = jnp.minimum(sizes[giver] - 1, bound - sizes[receiver]) // 2
    slack = jnp.where((giver == order[0]) | (receiver == order[0]) | (sizes[receiver] == 0), 0, jnp.maximum(slack, 0))
    passed = jax.random.randint(jax.random.fold_in(own, 4), (amount // 2,), 0, 1 << 20) % (slack + 1)
    sizes = sizes.at[giver].add(-passed).at[receiver].add(passed)
    labels = jnp.searchsorted(jnp.cumsum(sizes), jnp.arange(rows * top), side="right").astype(jnp.int32)
    listing = labels.reshape(top, rows).T
    listing = listing[jax.random.permutation(jax.random.fold_in(own, 1), rows)]
    rotation = jax.random.randint(jax.random.fold_in(own, 2), (rows, 1), 0, top)
    return jnp.take_along_axis(listing, (jnp.arange(top)[None, :] + rotation) % top, axis=1)


def shares(amount, total, bound, skew, full):
    portions = [(1 << 20) // math.isqrt(rank ** skew) + 1 for rank in range(1, amount + 1)]
    largest = bound if full else min(bound, max(-(-total // amount), total * portions[0] // sum(portions)))
    least = 1 if total - largest >= amount - 1 else 0
    holding, rest = [largest] + [least] * (amount - 1), total - largest - least * (amount - 1)
    while rest > 0:
        candidates = [i for i in range(1, amount) if holding[i] < largest] or [i for i in range(1, amount) if holding[i] < bound]
        pool, budget = sum([portions[i] for i in candidates]), rest
        for i in candidates:
            addition = min(bound - holding[i], max(1, budget * portions[i] // pool), rest)
            holding[i] = holding[i] + addition
            rest = rest - addition
    return np.array(holding)


def centred(rng, shape, spread, most, shards=(), kind=jnp.bfloat16):
    array = spread * jax.random.normal(rng, shape, jnp.float32)
    if shards:
        array = array * level_of(rng, shape, shards, -0.22, 0.18)
    return jnp.clip(array, -most, most).astype(kind)


def setup_inputs(seed: int = 0) -> dict:
    streams_of = jax.random.split(jax.random.key(seed), 5)
    points = centred(streams_of[0], (POINTS, D), 1.0, 6.0, ((0, 64), (1, 2)))
    owner_keys = jax.random.split(jax.random.fold_in(streams_of[1], 1), POINTS // PTS_DEV)
    owner_turns = jax.random.permutation(jax.random.fold_in(streams_of[1], 3), POINTS // PTS_DEV)
    owner = jax.vmap(lambda own, number: shared_out(jax.random.fold_in(streams_of[1], 2), own, number, PTS_DEV, N_BLK, 1, 2 * PTS_DEV // N_BLK, 2))(owner_keys, owner_turns).reshape((POINTS, 1))
    member = set_ends(jax.random.randint(streams_of[2], (POINTS,), 0, KC_DEV), jax.random.fold_in(streams_of[2], 1), 0, KC_DEV - 1).astype(jnp.int32)
    centroids = centred(streams_of[3], (LISTS, D), 0.5, 3.0, ((0, 64), (1, 2)))
    return dict(points=points, owner=owner, member=member, centroids=centroids)


def reference(points, owner, member, centroids):
    owners = owner[:, 0]
    point_floats = points.astype(jnp.float32)

    def block_update(index):
        target = jnp.where(owners == index, member, KC_DEV)
        sums = jnp.zeros((KC_DEV, D), jnp.float32).at[target].add(point_floats, mode="drop")
        counts = jnp.zeros((KC_DEV,), jnp.float32).at[target].add(jnp.ones(target.shape, jnp.float32), mode="drop")
        olds = lax.dynamic_slice_in_dim(centroids, (index * KC_DEV).astype(jnp.int32), KC_DEV, 0)
        return ((sums + olds.astype(jnp.float32)) / (counts[:, None] + 1.0)).astype(jnp.bfloat16)

    updated = lax.map(block_update, jnp.arange(N_BLK, dtype=jnp.int32))

    def block_nearest(index):
        rows = lax.dynamic_slice_in_dim(points, (index * PTS_DEV).astype(jnp.int32), PTS_DEV, 0)
        row_floats = rows.astype(jnp.float32)
        squares = jnp.sum(row_floats * row_floats, axis=1)
        best = jnp.full((PTS_DEV,), jnp.inf, jnp.float32)
        for section in range(CYCLE + 1):
            source = ((index - section) % N_BLK).astype(jnp.int32)
            candidate = updated[source]
            cand_floats = candidate.astype(jnp.float32)
            cand_squares = jnp.sum(cand_floats * cand_floats, axis=1)
            inner = lax.dot_general(rows, candidate, (((1,), (1,)), ((), ())), preferred_element_type=jnp.float32)
            distance = (squares[:, None] + cand_squares[None, :] - 2.0 * inner) / D
            best = jnp.minimum(best, jnp.min(distance, axis=1))
        return best

    nearest = lax.map(block_nearest, jnp.arange(N_BLK, dtype=jnp.int32))
    return updated.reshape(LISTS, D), nearest.reshape(POINTS)
```

```python
import functools

import jax
import jax.numpy as jnp
from jax import lax
from jax.experimental import pallas as pl
from jax.experimental.pallas import tpu as pltpu
from jax.sharding import PartitionSpec as P

D = 1024
CYCLE = 2
LANES = 128
META = 8
TILE = 256
CHUNKS = (1024, 1024, 1024, 512, 512)
COLS = 512
BF16 = jnp.bfloat16
F32 = jnp.float32
I32 = jnp.int32


def iota(shape, dim):
    return lax.broadcasted_iota(I32, shape, dim)


def pack_kernel(lane_ref, owner_ref, member_ref, pts_ref, out_ref, *, blocks, slots):
    count, width = pts_ref.shape
    tiles = width // LANES
    owner = owner_ref[...]
    is_owner = owner == iota((blocks, count), 0)
    weights = jnp.where(is_owner, 1.0, 0.0).astype(BF16)
    before = jnp.where(iota((count, count), 0) < iota((count, count), 1), 1.0, 0.0).astype(BF16)
    earlier = jnp.dot(weights, before, preferred_element_type=F32)
    place = jnp.sum(jnp.where(is_owner, earlier, 0.0), axis=0, keepdims=True).astype(I32)
    slot = owner * slots + place
    member = member_ref[...]
    lane = jnp.where(iota((LANES, count), 0) == place + lane_ref[0], 1.0, 0.0).astype(BF16)

    def spread(row):
        return lax.dot_general(
            jnp.where(is_owner, row.astype(F32), 0.0).astype(BF16),
            lane,
            (((1,), (1,)), ((), ())),
            preferred_element_type=F32,
        )

    high = spread((member >> 6) + 1)
    low = spread(member & 63)
    row = iota((blocks, META, LANES), 1)
    out_ref[:, slots * tiles :, :] = jnp.where(
        row == 0, high[:, None, :], jnp.where(row == 1, low[:, None, :], 0.0)
    ).astype(BF16)
    group = TILE // slots
    for g in range(blocks // group):
        pick = jnp.where(iota((TILE, count), 0) + g * TILE == slot, 1.0, 0.0).astype(BF16)
        placed = jnp.dot(pick, pts_ref[...], preferred_element_type=F32).astype(BF16)
        for o in range(group):
            for t in range(tiles):
                out_ref[g * group + o, t * slots : (t + 1) * slots, :] = placed[
                    o * slots : (o + 1) * slots, t * LANES : (t + 1) * LANES
                ]


def pack(lane, owner, member, points, blocks, slots):
    count, width = points.shape
    rows = slots * (width // LANES) + META
    vmem = pl.BlockSpec(memory_space=pltpu.VMEM)
    return pl.pallas_call(
        functools.partial(pack_kernel, blocks=blocks, slots=slots),
        out_shape=jax.ShapeDtypeStruct((blocks, rows, LANES), BF16),
        in_specs=[pl.BlockSpec(memory_space=pltpu.SMEM), vmem, vmem, vmem],
        out_specs=vmem,
        compiler_params=pltpu.CompilerParams(vmem_limit_bytes=24 << 20),
        cost_estimate=pl.CostEstimate(
            flops=2 * blocks * slots * count * width, bytes_accessed=6 << 20, transcendentals=0
        ),
        name="pack",
    )(lane, owner, member, points)


def update_kernel(first_ref, got_ref, old_ref, *refs, blocks, slots, chained):
    if chained:
        refs = refs[1:]
    out_ref, part_ref, rows_ref, list_ref = refs
    step = pl.program_id(0)
    width = old_ref.shape[1]
    tiles = width // LANES
    share = LANES // slots
    strips = blocks // share

    @pl.when(step == 0)
    def _():
        for o in range(blocks):
            for t in range(tiles):
                rows_ref[o * slots : (o + 1) * slots, t * LANES : (t + 1) * LANES] = got_ref[
                    o, t * slots : (t + 1) * slots, :
                ]
        meta = got_ref[:, slots * tiles :, :].astype(F32)
        row = iota(meta.shape, 1)
        number = jnp.sum(
            jnp.where(row == 0, meta * 64.0, jnp.where(row == 1, meta, 0.0)), axis=1
        )
        number = jnp.sum(number.reshape(strips, share, LANES), axis=1)
        list_ref[...] = number.astype(I32) - 64

    want = iota((TILE, LANES), 0) + (first_ref[0] + step) * TILE
    picks = []
    total = jnp.zeros((TILE, LANES), F32)
    for g in range(strips):
        hit = jnp.where(list_ref[g : g + 1, :] == want, 1.0, 0.0)
        total = total + hit
        picks.append(hit.astype(BF16))
    sums = jnp.dot(jnp.concatenate(picks, axis=1), rows_ref[...], preferred_element_type=F32)
    counts = jnp.sum(total, axis=1, keepdims=True)
    new = ((sums + old_ref[...].astype(F32)) / (counts + 1.0)).astype(BF16)
    out_ref[...] = new
    part_ref[...] = new


def update(first, got, centroids, so_far, count, blocks, slots):
    lists, width = centroids.shape
    tile = lambda i, first: (first[0] + i, 0)
    chained = so_far is not None
    in_specs = [
        pl.BlockSpec(got.shape, lambda i, first: (0, 0, 0), pipeline_mode=pl.Buffered(1)),
        pl.BlockSpec((TILE, width), tile),
    ]
    args = [first, got, centroids]
    if chained:
        in_specs.append(pl.BlockSpec(memory_space=pl.ANY))
        args.append(so_far)
    return pl.pallas_call(
        functools.partial(update_kernel, blocks=blocks, slots=slots, chained=chained),
        out_shape=(
            jax.ShapeDtypeStruct((lists, width), BF16),
            jax.ShapeDtypeStruct((count, width), BF16),
        ),
        grid_spec=pltpu.PrefetchScalarGridSpec(
            num_scalar_prefetch=1,
            grid=(count // TILE,),
            in_specs=in_specs,
            out_specs=(
                pl.BlockSpec((TILE, width), tile),
                pl.BlockSpec((TILE, width), lambda i, first: (i, 0)),
            ),
            scratch_shapes=[
                pltpu.VMEM((blocks * slots, width), BF16),
                pltpu.VMEM((blocks * slots // LANES, LANES), I32),
            ],
        ),
        input_output_aliases={3: 0} if chained else {},
        compiler_params=pltpu.CompilerParams(
            dimension_semantics=("arbitrary",), vmem_limit_bytes=24 << 20
        ),
        cost_estimate=pl.CostEstimate(
            flops=2 * count * blocks * slots * width,
            bytes_accessed=got.size * 2 + count * width * 6,
            transcendentals=0,
        ),
        name="update",
    )(*args)


def search_kernel(own_ref, other_ref, *refs, first, last):
    sections = CYCLE + 1
    points, refs = refs[: 2 * sections], refs[2 * sections :]
    if not first:
        before_ref, refs = refs[0], refs[1:]
    if last:
        outs, best_ref = refs[:sections], refs[sections]
    else:
        best_ref = refs[0]
    step = pl.program_id(0)
    count = points[0].shape[1]

    @pl.when(step == 0)
    def _():
        best_ref[...] = jnp.full_like(best_ref, -jnp.inf) if first else before_ref[...]

    own, other = own_ref[...], other_ref[...]
    own_f, other_f = own.astype(F32), other.astype(F32)
    half = 0.5 * (
        jnp.sum(own_f * own_f, axis=1, keepdims=True)
        + jnp.sum(other_f * other_f, axis=1, keepdims=True)
    )
    for s in range(sections):
        for c in range(0, count, COLS):
            score = jnp.dot(own, points[2 * s][:, c : c + COLS], preferred_element_type=F32)
            score += jnp.dot(other, points[2 * s + 1][:, c : c + COLS], preferred_element_type=F32)
            score -= half
            top = jnp.max(score.reshape(-1, 8, COLS), axis=0)
            at = slice(s * count + c, s * count + c + COLS)
            best_ref[:, at] = jnp.maximum(best_ref[:, at], top)

    if last:

        @pl.when(step == pl.num_programs(0) - 1)
        def _():
            for s in range(sections):
                outs[s][...] = jnp.max(
                    best_ref[:, s * count : (s + 1) * count], axis=0, keepdims=True
                )


def search(own, offset, other, points, before, last):
    chunk, width = other.shape
    sections = CYCLE + 1
    count = points[0].shape[1]
    tile = TILE if chunk % (2 * TILE) else 2 * TILE
    whole = lambda i: (0, 0)
    in_specs = [
        pl.BlockSpec((tile, width), lambda i: (i + offset // tile, 0)),
        pl.BlockSpec((tile, width), lambda i: (i, 0)),
    ]
    in_specs += [pl.BlockSpec((width, count), whole, pipeline_mode=pl.Buffered(1))] * len(points)
    args = [own, other, *points]
    best = (8, sections * count)
    if before is not None:
        in_specs.append(pl.BlockSpec(best, whole))
        args.append(before)
    scratch = []
    if last:
        out_shape = [jax.ShapeDtypeStruct((1, count), F32)] * sections
        out_specs = [pl.BlockSpec((1, count), whole)] * sections
        scratch = [pltpu.VMEM(best, F32)]
    else:
        out_shape = jax.ShapeDtypeStruct(best, F32)
        out_specs = pl.BlockSpec(best, whole)
    return pl.pallas_call(
        functools.partial(search_kernel, first=before is None, last=last),
        out_shape=out_shape,
        grid=(chunk // tile,),
        in_specs=in_specs,
        out_specs=out_specs,
        scratch_shapes=scratch,
        compiler_params=pltpu.CompilerParams(
            dimension_semantics=("arbitrary",), vmem_limit_bytes=28 << 20
        ),
        cost_estimate=pl.CostEstimate(
            flops=4 * chunk * width * sections * count,
            bytes_accessed=len(points) * width * count * 2 + chunk * width * 4,
            transcendentals=0,
        ),
        name="search",
    )(*args)


def shards(points, owner, member, centroids):
    lists, width = centroids.shape
    count = points.shape[0]
    blocks = lax.axis_size("blk")
    slots = 2 * count // blocks
    both = ("blk", "dim")
    mine = lax.axis_index("blk")
    side = lax.axis_index("dim")
    ids = [(b, d) for b in range(blocks) for d in range(2)]

    def fetch(x, source):
        route = []
        for b, d in ids:
            sb, sd = source(b, d)
            route.append(((sb % blocks) * 2 + sd, b * 2 + d))
        return lax.ppermute(x, both, route)

    lane = ((mine % (LANES // slots)) * slots).astype(I32).reshape(1)
    sent = pack(lane, owner.reshape(1, count), member.reshape(1, count), points, blocks, slots)
    got = lax.all_to_all(sent, "blk", split_axis=0, concat_axis=0, tiled=True)

    own_0 = points.T
    other_0 = fetch(own_0, lambda b, d: (b, 1 - d))
    own_2 = fetch(own_0, lambda b, d: (b + 2, d))
    other_2 = fetch(own_0, lambda b, d: (b + 2, 1 - d))
    even = mine % 2 == 0
    own_1 = fetch(jnp.where(even, own_2, own_0), lambda b, d: (b ^ 1, d))
    other_1 = fetch(jnp.where(even, other_2, other_0), lambda b, d: (b ^ 1, d))
    visitors = [own_0, other_0, own_1, other_1, own_2, other_2]
    squares = jnp.sum(jnp.square(own_0.astype(F32)), axis=0) + jnp.sum(
        jnp.square(other_0.astype(F32)), axis=0
    )

    half_tiles = lists // 2 // TILE
    new_centroids = None
    arrived = []
    done = 0
    for chunk in CHUNKS:
        first = ((1 - side) * half_tiles + done // TILE).astype(I32).reshape(1)
        new_centroids, part = update(first, got, centroids, new_centroids, chunk, blocks, slots)
        arrived.append(fetch(part, lambda b, d: (b, 1 - d)))
        done += chunk
    first = (side * half_tiles).astype(I32).reshape(1)
    new_centroids, own_half = update(
        first, got, centroids, new_centroids, lists // 2, blocks, slots
    )

    best = None
    done = 0
    for n, chunk in enumerate(CHUNKS):
        best = search(own_half, done, arrived[n], visitors, best, n == len(CHUNKS) - 1)
        done += chunk
    best = [x.reshape(count) for x in best]
    top = jnp.maximum(best[0], fetch(best[0], lambda b, d: (b, 1 - d)))
    for s in range(1, CYCLE + 1):
        for flip in (0, 1):
            top = jnp.maximum(top, fetch(best[s], lambda b, d: (b - s, d ^ flip)))
    nearest = (squares - 2.0 * top) / D
    return new_centroids, nearest


def solution(mesh):
    in_specs = (P("blk", "dim"), P("blk", None), P("blk"), P("blk", "dim"))
    out_specs = (P("blk", "dim"), P("blk"))
    return jax.shard_map(shards, mesh=mesh, in_specs=in_specs, out_specs=out_specs, check_vma=False)
```

```python
import functools

import jax
import jax.numpy as jnp
from jax import lax
from jax.experimental import pallas as pl
from jax.experimental.pallas import tpu as pltpu
from jax.sharding import PartitionSpec as P


D = 1024
CYCLE = 2
LANES = 128
META = 8
TILE = 256
CHUNKS = (1024, 1024, 1024, 512, 512)
COLS = 512
BF16 = jnp.bfloat16
F32 = jnp.float32
I32 = jnp.int32


def iota(shape, dim):
    return lax.broadcasted_iota(I32, shape, dim)


def pack_kernel(lane_ref, owner_ref, member_ref, pts_ref, out_ref, slot_ref, high_ref, low_ref, *, slots):
    count, width = pts_ref.shape
    tiles = width // LANES
    blocks = high_ref.shape[0]
    group = TILE // slots
    step = pl.program_id(0)

    @pl.when(step == 0)
    def _():
        owner = owner_ref[...]
        is_owner = owner == iota((blocks, count), 0)
        weights = jnp.where(is_owner, 1.0, 0.0).astype(BF16)
        before = jnp.where(iota((count, count), 0) < iota((count, count), 1), 1.0, 0.0)
        earlier = jnp.dot(weights, before.astype(BF16), preferred_element_type=F32)
        place = jnp.sum(jnp.where(is_owner, earlier, 0.0), axis=0, keepdims=True).astype(I32)
        slot_ref[...] = owner * slots + place
        member = member_ref[...]
        lane = jnp.where(iota((LANES, count), 0) == place + lane_ref[0], 1.0, 0.0).astype(BF16)

        def spread(row):
            return lax.dot_general(
                jnp.where(is_owner, row.astype(F32), 0.0).astype(BF16),
                lane,
                (((1,), (1,)), ((), ())),
                preferred_element_type=F32,
            )

        high_ref[...] = spread((member >> 6) + 1)
        low_ref[...] = spread(member & 63)

    row = iota((group, META, LANES), 1)
    mine = pl.ds(pl.multiple_of(step * group, group), group)
    high, low = high_ref[mine, :], low_ref[mine, :]
    out_ref[:, slots * tiles :, :] = jnp.where(
        row == 0, high[:, None, :], jnp.where(row == 1, low[:, None, :], 0.0)
    ).astype(BF16)
    pick = jnp.where(iota((TILE, count), 0) + step * TILE == slot_ref[...], 1.0, 0.0).astype(BF16)
    placed = jnp.dot(pick, pts_ref[...], preferred_element_type=F32).astype(BF16)
    for o in range(group):
        for t in range(tiles):
            out_ref[o, t * slots : (t + 1) * slots, :] = placed[
                o * slots : (o + 1) * slots, t * LANES : (t + 1) * LANES
            ]


def pack(lane, owner, member, points, blocks, slots):
    count, width = points.shape
    rows = slots * (width // LANES) + META
    group = TILE // slots
    whole = lambda i: (0, 0)
    return pl.pallas_call(
        functools.partial(pack_kernel, slots=slots),
        out_shape=jax.ShapeDtypeStruct((blocks, rows, LANES), BF16),
        grid=(blocks // group,),
        in_specs=[
            pl.BlockSpec(memory_space=pltpu.SMEM),
            pl.BlockSpec((1, count), whole),
            pl.BlockSpec((1, count), whole),
            pl.BlockSpec((count, width), whole),
        ],
        out_specs=pl.BlockSpec((group, rows, LANES), lambda i: (i, 0, 0)),
        scratch_shapes=[
            pltpu.VMEM((1, count), I32),
            pltpu.VMEM((blocks, LANES), F32),
            pltpu.VMEM((blocks, LANES), F32),
        ],
        compiler_params=pltpu.CompilerParams(
            dimension_semantics=("arbitrary",), vmem_limit_bytes=60 << 20
        ),
        cost_estimate=pl.CostEstimate(
            flops=2 * blocks * slots * count * width, bytes_accessed=6 << 20, transcendentals=0
        ),
        name="pack",
    )(lane, owner, member, points)


def update_kernel(first_ref, got_ref, old_ref, *refs, blocks, slots, chained):
    if chained:
        refs = refs[1:]
    out_ref, part_ref, rows_ref, list_ref = refs
    step = pl.program_id(0)
    width = old_ref.shape[1]
    tiles = width // LANES
    share = LANES // slots
    strips = blocks // share

    @pl.when(step == 0)
    def _():
        for o in range(blocks):
            for t in range(tiles):
                rows_ref[o * slots : (o + 1) * slots, t * LANES : (t + 1) * LANES] = got_ref[
                    o, t * slots : (t + 1) * slots, :
                ]
        meta = got_ref[:, slots * tiles :, :].astype(F32)
        row = iota(meta.shape, 1)
        number = jnp.sum(
            jnp.where(row == 0, meta * 64.0, jnp.where(row == 1, meta, 0.0)), axis=1
        )
        number = jnp.sum(number.reshape(strips, share, LANES), axis=1)
        list_ref[...] = number.astype(I32) - 64

    want = iota((TILE, LANES), 0) + (first_ref[0] + step) * TILE
    picks = []
    total = jnp.zeros((TILE, LANES), F32)
    for g in range(strips):
        hit = jnp.where(list_ref[g : g + 1, :] == want, 1.0, 0.0)
        total = total + hit
        picks.append(hit.astype(BF16))
    sums = jnp.dot(jnp.concatenate(picks, axis=1), rows_ref[...], preferred_element_type=F32)
    counts = jnp.sum(total, axis=1, keepdims=True)
    new = ((sums + old_ref[...].astype(F32)) / (counts + 1.0)).astype(BF16)
    out_ref[...] = new
    part_ref[...] = new


def update(first, got, centroids, so_far, count, blocks, slots):
    lists, width = centroids.shape
    tile = lambda i, first: (first[0] + i, 0)
    chained = so_far is not None
    in_specs = [
        pl.BlockSpec(got.shape, lambda i, first: (0, 0, 0), pipeline_mode=pl.Buffered(1)),
        pl.BlockSpec((TILE, width), tile),
    ]
    args = [first, got, centroids]
    if chained:
        in_specs.append(pl.BlockSpec(memory_space=pl.ANY))
        args.append(so_far)
    return pl.pallas_call(
        functools.partial(update_kernel, blocks=blocks, slots=slots, chained=chained),
        out_shape=(
            jax.ShapeDtypeStruct((lists, width), BF16),
            jax.ShapeDtypeStruct((count, width), BF16),
        ),
        grid_spec=pltpu.PrefetchScalarGridSpec(
            num_scalar_prefetch=1,
            grid=(count // TILE,),
            in_specs=in_specs,
            out_specs=(
                pl.BlockSpec((TILE, width), tile),
                pl.BlockSpec((TILE, width), lambda i, first: (i, 0)),
            ),
            scratch_shapes=[
                pltpu.VMEM((blocks * slots, width), BF16),
                pltpu.VMEM((blocks * slots // LANES, LANES), I32),
            ],
        ),
        input_output_aliases={3: 0} if chained else {},
        compiler_params=pltpu.CompilerParams(
            dimension_semantics=("arbitrary",), vmem_limit_bytes=24 << 20
        ),
        cost_estimate=pl.CostEstimate(
            flops=2 * count * blocks * slots * width,
            bytes_accessed=got.size * 2 + count * width * 6,
            transcendentals=0,
        ),
        name="update",
    )(*args)


def search_kernel(own_ref, other_ref, *refs, first, last):
    sections = CYCLE + 1
    points, refs = refs[: 2 * sections], refs[2 * sections :]
    if not first:
        before_ref, refs = refs[0], refs[1:]
    if last:
        outs, best_ref = refs[:sections], refs[sections]
    else:
        best_ref = refs[0]
    step = pl.program_id(0)
    count = points[0].shape[1]

    @pl.when(step == 0)
    def _():
        best_ref[...] = jnp.full_like(best_ref, -jnp.inf) if first else before_ref[...]

    own, other = own_ref[...], other_ref[...]
    own_f, other_f = own.astype(F32), other.astype(F32)
    half = 0.5 * (
        jnp.sum(own_f * own_f, axis=1, keepdims=True)
        + jnp.sum(other_f * other_f, axis=1, keepdims=True)
    )
    for s in range(sections):
        for c in range(0, count, COLS):
            score = jnp.dot(own, points[2 * s][:, c : c + COLS], preferred_element_type=F32)
            score += jnp.dot(other, points[2 * s + 1][:, c : c + COLS], preferred_element_type=F32)
            score -= half
            top = jnp.max(score.reshape(-1, 8, COLS), axis=0)
            at = slice(s * count + c, s * count + c + COLS)
            best_ref[:, at] = jnp.maximum(best_ref[:, at], top)

    if last:

        @pl.when(step == pl.num_programs(0) - 1)
        def _():
            for s in range(sections):
                outs[s][...] = jnp.max(
                    best_ref[:, s * count : (s + 1) * count], axis=0, keepdims=True
                )


def search(own, offset, other, points, before, last):
    chunk, width = other.shape
    sections = CYCLE + 1
    count = points[0].shape[1]
    tile = TILE if chunk % (2 * TILE) else 2 * TILE
    whole = lambda i: (0, 0)
    in_specs = [
        pl.BlockSpec((tile, width), lambda i: (i + offset // tile, 0)),
        pl.BlockSpec((tile, width), lambda i: (i, 0)),
    ]
    in_specs += [pl.BlockSpec((width, count), whole, pipeline_mode=pl.Buffered(1))] * len(points)
    args = [own, other, *points]
    best = (8, sections * count)
    if before is not None:
        in_specs.append(pl.BlockSpec(best, whole))
        args.append(before)
    scratch = []
    if last:
        out_shape = [jax.ShapeDtypeStruct((1, count), F32)] * sections
        out_specs = [pl.BlockSpec((1, count), whole)] * sections
        scratch = [pltpu.VMEM(best, F32)]
    else:
        out_shape = jax.ShapeDtypeStruct(best, F32)
        out_specs = pl.BlockSpec(best, whole)
    return pl.pallas_call(
        functools.partial(search_kernel, first=before is None, last=last),
        out_shape=out_shape,
        grid=(chunk // tile,),
        in_specs=in_specs,
        out_specs=out_specs,
        scratch_shapes=scratch,
        compiler_params=pltpu.CompilerParams(
            dimension_semantics=("arbitrary",), vmem_limit_bytes=28 << 20
        ),
        cost_estimate=pl.CostEstimate(
            flops=4 * chunk * width * sections * count,
            bytes_accessed=len(points) * width * count * 2 + chunk * width * 4,
            transcendentals=0,
        ),
        name="search",
    )(*args)


def step(points, owner, member, centroids):
    lists, width = centroids.shape
    count = points.shape[0]
    blocks = lax.axis_size("blk")
    slots = 2 * count // blocks
    both = ("blk", "dim")
    mine = lax.axis_index("blk")
    side = lax.axis_index("dim")
    ids = [(b, d) for b in range(blocks) for d in range(2)]

    def fetch(x, source):
        route = []
        for b, d in ids:
            sb, sd = source(b, d)
            route.append(((sb % blocks) * 2 + sd, b * 2 + d))
        return lax.ppermute(x, both, route)

    near_own = fetch(points, lambda b, d: (b ^ 2, d))
    near_other = fetch(points, lambda b, d: (b ^ 2, 1 - d))

    lane = ((mine % (LANES // slots)) * slots).astype(I32).reshape(1)
    sent = pack(lane, owner.reshape(1, count), member.reshape(1, count), points, blocks, slots)
    got = lax.all_to_all(sent, "blk", split_axis=0, concat_axis=0, tiled=True)

    own_0 = points.T
    near_own, near_other = near_own.T, near_other.T
    part = width // 2
    first_part = fetch(near_other[:part], lambda b, d: (b ^ 2, d))
    second_part = fetch(near_own[part:], lambda b, d: (b ^ 2, 1 - d))
    onward = lambda b, d: (b + 4 if b & 2 else b, d)
    own_2 = fetch(near_own, onward)
    other_2 = fetch(near_other, onward)
    other_0 = jnp.concatenate([first_part, second_part], axis=0)
    even = mine % 2 == 0
    own_1 = fetch(jnp.where(even, own_2, own_0), lambda b, d: (b ^ 1, d))
    other_1 = fetch(jnp.where(even, other_2, other_0), lambda b, d: (b ^ 1, d))
    visitors = [own_0, other_0, own_1, other_1, own_2, other_2]
    squares = jnp.sum(jnp.square(own_0.astype(F32)), axis=0) + jnp.sum(
        jnp.square(other_0.astype(F32)), axis=0
    )

    old = pltpu.with_memory_space_constraint(centroids, pltpu.HBM)
    half_tiles = lists // 2 // TILE
    new_centroids = None
    arrived = []
    done = 0
    for chunk in CHUNKS:
        first = ((1 - side) * half_tiles + done // TILE).astype(I32).reshape(1)
        new_centroids, part = update(first, got, old, new_centroids, chunk, blocks, slots)
        arrived.append(fetch(part, lambda b, d: (b, 1 - d)))
        done += chunk
    first = (side * half_tiles).astype(I32).reshape(1)
    new_centroids, own_half = update(
        first, got, old, new_centroids, lists // 2, blocks, slots
    )

    best = None
    done = 0
    for n, chunk in enumerate(CHUNKS):
        best = search(own_half, done, arrived[n], visitors, best, n == len(CHUNKS) - 1)
        done += chunk
    best = [x.reshape(count) for x in best]
    top = jnp.maximum(best[0], fetch(best[0], lambda b, d: (b, 1 - d)))
    for s in range(1, CYCLE + 1):
        for flip in (0, 1):
            top = jnp.maximum(top, fetch(best[s], lambda b, d: (b - s, d ^ flip)))
    nearest = (squares - 2.0 * top) / D
    return new_centroids, nearest


def solution(mesh):
    in_specs = (P("blk", "dim"), P("blk", None), P("blk"), P("blk", "dim"))
    out_specs = (P("blk", "dim"), P("blk"))
    return jax.shard_map(step, mesh=mesh, in_specs=in_specs, out_specs=out_specs, check_vma=False)
```

```python
import functools

import jax
import jax.numpy as jnp
from jax import lax
from jax.experimental import pallas as pl
from jax.experimental.pallas import tpu as pltpu
from jax.sharding import PartitionSpec as P


D = 1024
CYCLE = 2
LANES = 128
META = 8
TILE = 256
CHUNKS = (512, 1024, 1024, 1024, 512)
COLS = 512
PACK_STEPS = 2
BF16 = jnp.bfloat16
F32 = jnp.float32
I32 = jnp.int32


def iota(shape, dim):
    return lax.broadcasted_iota(I32, shape, dim)


def pack_kernel(lane_ref, owner_ref, member_ref, pts_ref, out_ref, slot_ref, high_ref, low_ref, *, slots):
    count, width = pts_ref.shape
    tiles = width // LANES
    blocks = high_ref.shape[0]
    group = out_ref.shape[0]
    step = pl.program_id(0)

    @pl.when(step == 0)
    def _():
        owner = owner_ref[...]
        is_owner = owner == iota((blocks, count), 0)
        weights = jnp.where(is_owner, 1.0, 0.0).astype(BF16)
        before = jnp.where(iota((count, count), 0) < iota((count, count), 1), 1.0, 0.0)
        earlier = jnp.dot(weights, before.astype(BF16), preferred_element_type=F32)
        place = jnp.sum(jnp.where(is_owner, earlier, 0.0), axis=0, keepdims=True).astype(I32)
        slot_ref[...] = owner * slots + place
        member = member_ref[...]
        lane = jnp.where(iota((LANES, count), 0) == place + lane_ref[0], 1.0, 0.0).astype(BF16)

        def spread(row):
            return lax.dot_general(
                jnp.where(is_owner, row.astype(F32), 0.0).astype(BF16),
                lane,
                (((1,), (1,)), ((), ())),
                preferred_element_type=F32,
            )

        high_ref[...] = spread((member >> 6) + 1)
        low_ref[...] = spread(member & 63)

    row = iota((group, META, LANES), 1)
    mine = pl.ds(pl.multiple_of(step * group, group), group)
    high, low = high_ref[mine, :], low_ref[mine, :]
    out_ref[:, slots * tiles :, :] = jnp.where(
        row == 0, high[:, None, :], jnp.where(row == 1, low[:, None, :], 0.0)
    ).astype(BF16)
    part = TILE // slots
    for p in range(group // part):
        want = iota((TILE, count), 0) + (step * group + p * part) * slots
        pick = jnp.where(want == slot_ref[...], 1.0, 0.0).astype(BF16)
        placed = jnp.dot(pick, pts_ref[...], preferred_element_type=F32).astype(BF16)
        for o in range(part):
            for t in range(tiles):
                out_ref[p * part + o, t * slots : (t + 1) * slots, :] = placed[
                    o * slots : (o + 1) * slots, t * LANES : (t + 1) * LANES
                ]


def pack(lane, owner, member, points, blocks, slots):
    count, width = points.shape
    rows = slots * (width // LANES) + META
    group = blocks // PACK_STEPS
    whole = lambda i: (0, 0)
    return pl.pallas_call(
        functools.partial(pack_kernel, slots=slots),
        out_shape=jax.ShapeDtypeStruct((blocks, rows, LANES), BF16),
        grid=(blocks // group,),
        in_specs=[
            pl.BlockSpec(memory_space=pltpu.SMEM),
            pl.BlockSpec((1, count), whole),
            pl.BlockSpec((1, count), whole),
            pl.BlockSpec((count, width), whole),
        ],
        out_specs=pl.BlockSpec((group, rows, LANES), lambda i: (i, 0, 0)),
        scratch_shapes=[
            pltpu.VMEM((1, count), I32),
            pltpu.VMEM((blocks, LANES), F32),
            pltpu.VMEM((blocks, LANES), F32),
        ],
        compiler_params=pltpu.CompilerParams(
            dimension_semantics=("arbitrary",), vmem_limit_bytes=60 << 20
        ),
        cost_estimate=pl.CostEstimate(
            flops=2 * blocks * slots * count * width, bytes_accessed=6 << 20, transcendentals=0
        ),
        name="pack",
    )(lane, owner, member, points)


def update_kernel(first_ref, got_ref, old_ref, *refs, blocks, slots, chained):
    if chained:
        refs = refs[1:]
    out_ref, part_ref, rows_ref, list_ref = refs
    step = pl.program_id(0)
    width = old_ref.shape[1]
    tiles = width // LANES
    share = LANES // slots
    strips = blocks // share

    @pl.when(step == 0)
    def _():
        for o in range(blocks):
            for t in range(tiles):
                rows_ref[o * slots : (o + 1) * slots, t * LANES : (t + 1) * LANES] = got_ref[
                    o, t * slots : (t + 1) * slots, :
                ]
        meta = got_ref[:, slots * tiles :, :].astype(F32)
        row = iota(meta.shape, 1)
        number = jnp.sum(
            jnp.where(row == 0, meta * 64.0, jnp.where(row == 1, meta, 0.0)), axis=1
        )
        number = jnp.sum(number.reshape(strips, share, LANES), axis=1)
        list_ref[...] = number.astype(I32) - 64

    want = iota((TILE, LANES), 0) + (first_ref[0] + step) * TILE
    picks = []
    total = jnp.zeros((TILE, LANES), F32)
    for g in range(strips):
        hit = jnp.where(list_ref[g : g + 1, :] == want, 1.0, 0.0)
        total = total + hit
        picks.append(hit.astype(BF16))
    sums = jnp.dot(jnp.concatenate(picks, axis=1), rows_ref[...], preferred_element_type=F32)
    counts = jnp.sum(total, axis=1, keepdims=True)
    new = ((sums + old_ref[...].astype(F32)) / (counts + 1.0)).astype(BF16)
    out_ref[...] = new
    part_ref[...] = new


def update(first, got, centroids, so_far, count, blocks, slots):
    lists, width = centroids.shape
    tile = lambda i, first: (first[0] + i, 0)
    chained = so_far is not None
    in_specs = [
        pl.BlockSpec(got.shape, lambda i, first: (0, 0, 0), pipeline_mode=pl.Buffered(1)),
        pl.BlockSpec((TILE, width), tile),
    ]
    args = [first, got, centroids]
    if chained:
        in_specs.append(pl.BlockSpec(memory_space=pl.ANY))
        args.append(so_far)
    return pl.pallas_call(
        functools.partial(update_kernel, blocks=blocks, slots=slots, chained=chained),
        out_shape=(
            jax.ShapeDtypeStruct((lists, width), BF16),
            jax.ShapeDtypeStruct((count, width), BF16),
        ),
        grid_spec=pltpu.PrefetchScalarGridSpec(
            num_scalar_prefetch=1,
            grid=(count // TILE,),
            in_specs=in_specs,
            out_specs=(
                pl.BlockSpec((TILE, width), tile),
                pl.BlockSpec((TILE, width), lambda i, first: (i, 0)),
            ),
            scratch_shapes=[
                pltpu.VMEM((blocks * slots, width), BF16),
                pltpu.VMEM((blocks * slots // LANES, LANES), I32),
            ],
        ),
        input_output_aliases={3: 0} if chained else {},
        compiler_params=pltpu.CompilerParams(
            dimension_semantics=("arbitrary",), vmem_limit_bytes=24 << 20
        ),
        cost_estimate=pl.CostEstimate(
            flops=2 * count * blocks * slots * width,
            bytes_accessed=got.size * 2 + count * width * 6,
            transcendentals=0,
        ),
        name="update",
    )(*args)


def search_kernel(own_ref, other_ref, *refs, first, last):
    sections = CYCLE + 1
    points, refs = refs[: 2 * sections], refs[2 * sections :]
    if not first:
        before_ref, refs = refs[0], refs[1:]
    if last:
        outs, best_ref = refs[:sections], refs[sections]
    else:
        best_ref = refs[0]
    step = pl.program_id(0)
    count = points[0].shape[1]

    @pl.when(step == 0)
    def _():
        best_ref[...] = jnp.full_like(best_ref, -jnp.inf) if first else before_ref[...]

    own, other = own_ref[...], other_ref[...]
    own_f, other_f = own.astype(F32), other.astype(F32)
    half = 0.5 * (
        jnp.sum(own_f * own_f, axis=1, keepdims=True)
        + jnp.sum(other_f * other_f, axis=1, keepdims=True)
    )
    for s in range(sections):
        for c in range(0, count, COLS):
            score = jnp.dot(own, points[2 * s][:, c : c + COLS], preferred_element_type=F32)
            score += jnp.dot(other, points[2 * s + 1][:, c : c + COLS], preferred_element_type=F32)
            score -= half
            top = jnp.max(score.reshape(-1, 8, COLS), axis=0)
            at = slice(s * count + c, s * count + c + COLS)
            best_ref[:, at] = jnp.maximum(best_ref[:, at], top)

    if last:

        @pl.when(step == pl.num_programs(0) - 1)
        def _():
            for s in range(sections):
                outs[s][...] = jnp.max(
                    best_ref[:, s * count : (s + 1) * count], axis=0, keepdims=True
                )


def search(own, offset, other, points, before, last):
    chunk, width = other.shape
    sections = CYCLE + 1
    count = points[0].shape[1]
    tile = TILE if chunk % (2 * TILE) else 2 * TILE
    whole = lambda i: (0, 0)
    in_specs = [
        pl.BlockSpec((tile, width), lambda i: (i + offset // tile, 0)),
        pl.BlockSpec((tile, width), lambda i: (i, 0)),
    ]
    in_specs += [pl.BlockSpec((width, count), whole, pipeline_mode=pl.Buffered(1))] * len(points)
    args = [own, other, *points]
    best = (8, sections * count)
    if before is not None:
        in_specs.append(pl.BlockSpec(best, whole))
        args.append(before)
    scratch = []
    if last:
        out_shape = [jax.ShapeDtypeStruct((1, count), F32)] * sections
        out_specs = [pl.BlockSpec((1, count), whole)] * sections
        scratch = [pltpu.VMEM(best, F32)]
    else:
        out_shape = jax.ShapeDtypeStruct(best, F32)
        out_specs = pl.BlockSpec(best, whole)
    return pl.pallas_call(
        functools.partial(search_kernel, first=before is None, last=last),
        out_shape=out_shape,
        grid=(chunk // tile,),
        in_specs=in_specs,
        out_specs=out_specs,
        scratch_shapes=scratch,
        compiler_params=pltpu.CompilerParams(
            dimension_semantics=("arbitrary",), vmem_limit_bytes=28 << 20
        ),
        cost_estimate=pl.CostEstimate(
            flops=4 * chunk * width * sections * count,
            bytes_accessed=len(points) * width * count * 2 + chunk * width * 4,
            transcendentals=0,
        ),
        name="search",
    )(*args)


def step(points, owner, member, centroids):
    lists, width = centroids.shape
    count = points.shape[0]
    blocks = lax.axis_size("blk")
    slots = 2 * count // blocks
    both = ("blk", "dim")
    mine = lax.axis_index("blk")
    side = lax.axis_index("dim")
    ids = [(b, d) for b in range(blocks) for d in range(2)]

    def fetch(x, source, odd=False):
        route = []
        for b, d in ids:
            if odd and not b & 2:
                continue
            sb, sd = source(b, d)
            route.append(((sb % blocks) * 2 + sd, b * 2 + d))
        return lax.ppermute(x, both, route)

    near_own = fetch(points, lambda b, d: (b ^ 2, d))
    near_other = fetch(points, lambda b, d: (b ^ 2, 1 - d))

    lane = ((mine % (LANES // slots)) * slots).astype(I32).reshape(1)
    sent = pack(lane, owner.reshape(1, count), member.reshape(1, count), points, blocks, slots)
    got = lax.all_to_all(sent, "blk", split_axis=0, concat_axis=0, tiled=True)

    own_0 = points.T
    near_own, near_other = near_own.T, near_other.T
    part = width // 2
    first_part = fetch(near_other[:part], lambda b, d: (b ^ 2, d))
    second_part = fetch(near_own[part:], lambda b, d: (b ^ 2, 1 - d))
    far = lambda b, d: (b + 4, d)
    odd = (mine // 2) % 2 == 1
    own_2 = jnp.where(odd, fetch(near_own, far, odd=True), near_own)
    other_2 = jnp.where(odd, fetch(near_other, far, odd=True), near_other)
    other_0 = jnp.concatenate([first_part, second_part], axis=0)
    even = mine % 2 == 0
    own_1 = fetch(jnp.where(even, own_2, own_0), lambda b, d: (b ^ 1, d))
    other_1 = fetch(jnp.where(even, other_2, other_0), lambda b, d: (b ^ 1, d))
    visitors = [own_0, other_0, own_1, other_1, own_2, other_2]
    squares = jnp.sum(jnp.square(own_0.astype(F32)), axis=0) + jnp.sum(
        jnp.square(other_0.astype(F32)), axis=0
    )

    old = pltpu.with_memory_space_constraint(centroids, pltpu.HBM)
    half_tiles = lists // 2 // TILE
    new_centroids = None
    arrived = []
    done = 0
    for chunk in CHUNKS:
        first = ((1 - side) * half_tiles + done // TILE).astype(I32).reshape(1)
        new_centroids, part = update(first, got, old, new_centroids, chunk, blocks, slots)
        arrived.append(fetch(part, lambda b, d: (b, 1 - d)))
        done += chunk
    first = (side * half_tiles).astype(I32).reshape(1)
    new_centroids, own_half = update(
        first, got, old, new_centroids, lists // 2, blocks, slots
    )

    best = None
    done = 0
    for n, chunk in enumerate(CHUNKS):
        best = search(own_half, done, arrived[n], visitors, best, n == len(CHUNKS) - 1)
        done += chunk
    best = [x.reshape(count) for x in best]
    top = jnp.maximum(best[0], fetch(best[0], lambda b, d: (b, 1 - d)))
    for s in range(1, CYCLE + 1):
        for flip in (0, 1):
            top = jnp.maximum(top, fetch(best[s], lambda b, d: (b - s, d ^ flip)))
    nearest = (squares - 2.0 * top) / D
    return new_centroids, nearest


def solution(mesh):
    in_specs = (P("blk", "dim"), P("blk", None), P("blk"), P("blk", "dim"))
    out_specs = (P("blk", "dim"), P("blk"))
    return jax.shard_map(step, mesh=mesh, in_specs=in_specs, out_specs=out_specs, check_vma=False)
```

```python
import functools

import jax
import jax.numpy as jnp
from jax import lax
from jax.experimental import pallas as pl
from jax.experimental.pallas import tpu as pltpu
from jax.sharding import PartitionSpec as P


D = 1024
CYCLE = 2
LANES = 128
META = 8
TILE = 256
CHUNKS = (512, 1024, 1024, 512, 512, 256, 256)
COLS = 512
PACK_STEPS = 2
BF16 = jnp.bfloat16
F32 = jnp.float32
I32 = jnp.int32


def iota(shape, dim):
    return lax.broadcasted_iota(I32, shape, dim)


def pack_kernel(
    lane_ref, plane_ref, block_ref, member_ref, pts_ref, out_ref, slot_ref, high_ref, low_ref, *, slots
):
    count, width = pts_ref.shape
    tiles = width // LANES
    owners = high_ref.shape[0]
    group = out_ref.shape[0]
    step = pl.program_id(0)

    @pl.when(step == 0)
    def _():
        block = block_ref[...]
        member = member_ref[...]
        here = ((block >> 1) & 1) == plane_ref[0]
        owner = jnp.where(here, (block >> 2) * 2 + (block & 1), -1)
        is_owner = owner == iota((owners, count), 0)
        weights = jnp.where(is_owner, 1.0, 0.0)
        before = jnp.where(iota((LANES, LANES), 0) < iota((LANES, LANES), 1), 1.0, 0.0).astype(BF16)
        earlier = []
        base = jnp.zeros((owners, 1), F32)
        for c in range(0, count, LANES):
            strip = weights[:, c : c + LANES]
            earlier.append(
                base + jnp.dot(strip.astype(BF16), before, preferred_element_type=F32)
            )
            base = base + jnp.sum(strip, axis=1, keepdims=True)
        earlier = jnp.concatenate(earlier, axis=1)
        place = jnp.sum(jnp.where(is_owner, earlier, 0.0), axis=0, keepdims=True).astype(I32)
        slot_ref[...] = jnp.where(here, owner * slots + place, -1)
        lane = jnp.where(iota((LANES, count), 0) == place + lane_ref[0], 1.0, 0.0).astype(BF16)

        def spread(row):
            return lax.dot_general(
                jnp.where(is_owner, row.astype(F32), 0.0).astype(BF16),
                lane,
                (((1,), (1,)), ((), ())),
                preferred_element_type=F32,
            )

        high_ref[...] = spread((member >> 6) + 1)
        low_ref[...] = spread(member & 63)

    row = iota((group, META, LANES), 1)
    mine = pl.ds(pl.multiple_of(step * group, group), group)
    high, low = high_ref[mine, :], low_ref[mine, :]
    out_ref[:, slots * tiles :, :] = jnp.where(
        row == 0, high[:, None, :], jnp.where(row == 1, low[:, None, :], 0.0)
    ).astype(BF16)
    part = TILE // slots
    for p in range(group // part):
        want = iota((TILE, count), 0) + (step * group + p * part) * slots
        pick = jnp.where(want == slot_ref[...], 1.0, 0.0).astype(BF16)
        placed = jnp.dot(pick, pts_ref[...], preferred_element_type=F32).astype(BF16)
        for o in range(part):
            for t in range(tiles):
                out_ref[p * part + o, t * slots : (t + 1) * slots, :] = placed[
                    o * slots : (o + 1) * slots, t * LANES : (t + 1) * LANES
                ]


def pack(lane, plane, block, member, points, owners, slots):
    count, width = points.shape
    rows = slots * (width // LANES) + META
    group = owners // PACK_STEPS
    whole = lambda i: (0, 0)
    return pl.pallas_call(
        functools.partial(pack_kernel, slots=slots),
        out_shape=jax.ShapeDtypeStruct((owners, rows, LANES), BF16),
        grid=(PACK_STEPS,),
        in_specs=[
            pl.BlockSpec(memory_space=pltpu.SMEM),
            pl.BlockSpec(memory_space=pltpu.SMEM),
            pl.BlockSpec((1, count), whole),
            pl.BlockSpec((1, count), whole),
            pl.BlockSpec((count, width), whole),
        ],
        out_specs=pl.BlockSpec((group, rows, LANES), lambda i: (i, 0, 0)),
        scratch_shapes=[
            pltpu.VMEM((1, count), I32),
            pltpu.VMEM((owners, LANES), F32),
            pltpu.VMEM((owners, LANES), F32),
        ],
        compiler_params=pltpu.CompilerParams(
            dimension_semantics=("arbitrary",), vmem_limit_bytes=60 << 20
        ),
        cost_estimate=pl.CostEstimate(
            flops=2 * owners * slots * count * width, bytes_accessed=4 << 20, transcendentals=0
        ),
        name="pack",
    )(lane, plane, block, member, points)


def update_kernel(first_ref, got_a_ref, got_b_ref, old_ref, *refs, owners, slots, chained):
    if chained:
        refs = refs[1:]
    out_ref, part_ref, rows_ref, list_ref = refs
    step = pl.program_id(0)
    size, width = old_ref.shape
    tiles = width // LANES
    share = LANES // slots
    strips = owners // share

    @pl.when(step == 0)
    def _():
        for n, got_ref in enumerate((got_a_ref, got_b_ref)):

            @pl.loop(0, owners, unroll=4)
            def _(o, n=n, got_ref=got_ref):
                at = pl.ds(pl.multiple_of((n * owners + o) * slots, slots), slots)
                for t in range(tiles):
                    rows_ref[at, t * LANES : (t + 1) * LANES] = got_ref[
                        o, t * slots : (t + 1) * slots, :
                    ]

            meta = got_ref[:, slots * tiles :, :].astype(F32)
            row = iota(meta.shape, 1)
            number = jnp.sum(
                jnp.where(row == 0, meta * 64.0, jnp.where(row == 1, meta, 0.0)), axis=1
            )
            number = jnp.sum(number.reshape(strips, share, LANES), axis=1)
            list_ref[n * strips : (n + 1) * strips, :] = number.astype(I32) - 64

    want = iota((size, LANES), 0) + (first_ref[0] + step) * size
    picks = []
    total = jnp.zeros((size, LANES), F32)
    for g in range(2 * strips):
        hit = jnp.where(list_ref[g : g + 1, :] == want, 1.0, 0.0)
        total = total + hit
        picks.append(hit.astype(BF16))
    sums = jnp.dot(jnp.concatenate(picks, axis=1), rows_ref[...], preferred_element_type=F32)
    counts = jnp.sum(total, axis=1, keepdims=True)
    new = ((sums + old_ref[...].astype(F32)) / (counts + 1.0)).astype(BF16)
    out_ref[...] = new
    part_ref[...] = new


def update(first, got, centroids, so_far, count, slots, size=TILE):
    lists, width = centroids.shape
    owners = got[0].shape[0]
    tile = lambda i, first: (first[0] + i, 0)
    chained = so_far is not None
    in_specs = [
        pl.BlockSpec(x.shape, lambda i, first: (0, 0, 0), pipeline_mode=pl.Buffered(1)) for x in got
    ]
    in_specs.append(pl.BlockSpec((size, width), tile))
    args = [first, *got, centroids]
    if chained:
        in_specs.append(pl.BlockSpec(memory_space=pl.ANY))
        args.append(so_far)
    return pl.pallas_call(
        functools.partial(update_kernel, owners=owners, slots=slots, chained=chained),
        out_shape=(
            jax.ShapeDtypeStruct((lists, width), BF16),
            jax.ShapeDtypeStruct((count, width), BF16),
        ),
        grid_spec=pltpu.PrefetchScalarGridSpec(
            num_scalar_prefetch=1,
            grid=(count // size,),
            in_specs=in_specs,
            out_specs=(
                pl.BlockSpec((size, width), tile),
                pl.BlockSpec((size, width), lambda i, first: (i, 0)),
            ),
            scratch_shapes=[
                pltpu.VMEM((2 * owners * slots, width), BF16),
                pltpu.VMEM((2 * owners * slots // LANES, LANES), I32),
            ],
        ),
        input_output_aliases={4: 0} if chained else {},
        compiler_params=pltpu.CompilerParams(
            dimension_semantics=("arbitrary",), vmem_limit_bytes=24 << 20
        ),
        cost_estimate=pl.CostEstimate(
            flops=4 * count * owners * slots * width,
            bytes_accessed=got[0].size * 4 + count * width * 6,
            transcendentals=0,
        ),
        name="update",
    )(*args)


def turn_kernel(*refs):
    out_ref = refs[-1]
    at = 0
    for ref in refs[:-1]:
        rows = ref.shape[0]
        out_ref[:, at : at + rows] = ref[...].T
        at += rows


def turn(*parts):
    width = parts[0].shape[1]
    half = width // 2
    count = sum(x.shape[0] for x in parts)
    return pl.pallas_call(
        turn_kernel,
        out_shape=jax.ShapeDtypeStruct((width, count), BF16),
        grid=(2,),
        in_specs=[pl.BlockSpec((x.shape[0], half), lambda i: (0, i)) for x in parts],
        out_specs=pl.BlockSpec((half, count), lambda i: (i, 0)),
        compiler_params=pltpu.CompilerParams(
            dimension_semantics=("arbitrary",), vmem_limit_bytes=24 << 20
        ),
        cost_estimate=pl.CostEstimate(
            flops=0, bytes_accessed=4 * width * count, transcendentals=0
        ),
        name="turn",
    )(*parts)


def search_kernel(own_ref, other_ref, *refs, first, last):
    sections = CYCLE + 1
    points, refs = refs[: 2 * sections], refs[2 * sections :]
    if not first:
        before_ref, refs = refs[0], refs[1:]
    if last:
        outs, best_ref = refs[:sections], refs[sections]
    else:
        best_ref = refs[0]
    step = pl.program_id(0)
    count = points[0].shape[1]

    @pl.when(step == 0)
    def _():
        best_ref[...] = jnp.full_like(best_ref, -jnp.inf) if first else before_ref[...]

    own, other = own_ref[...], other_ref[...]
    own_f, other_f = own.astype(F32), other.astype(F32)
    half = 0.5 * (
        jnp.sum(own_f * own_f, axis=1, keepdims=True)
        + jnp.sum(other_f * other_f, axis=1, keepdims=True)
    )
    for s in range(sections):
        for c in range(0, count, COLS):
            score = jnp.dot(own, points[2 * s][:, c : c + COLS], preferred_element_type=F32)
            score += jnp.dot(other, points[2 * s + 1][:, c : c + COLS], preferred_element_type=F32)
            score -= half
            top = jnp.max(score.reshape(-1, 8, COLS), axis=0)
            at = slice(s * count + c, s * count + c + COLS)
            best_ref[:, at] = jnp.maximum(best_ref[:, at], top)

    if last:

        @pl.when(step == pl.num_programs(0) - 1)
        def _():
            for s in range(sections):
                outs[s][...] = jnp.max(
                    best_ref[:, s * count : (s + 1) * count], axis=0, keepdims=True
                )


def search(own, offset, other, points, before, last):
    chunk, width = other.shape
    sections = CYCLE + 1
    count = points[0].shape[1]
    tile = TILE if chunk % (4 * TILE) else 2 * TILE
    whole = lambda i: (0, 0)
    in_specs = [
        pl.BlockSpec((tile, width), lambda i: (i + offset // tile, 0)),
        pl.BlockSpec((tile, width), lambda i: (i, 0)),
    ]
    in_specs += [pl.BlockSpec((width, count), whole, pipeline_mode=pl.Buffered(1))] * len(points)
    args = [own, other, *points]
    best = (8, sections * count)
    if before is not None:
        in_specs.append(pl.BlockSpec(best, whole))
        args.append(before)
    scratch = []
    if last:
        out_shape = [jax.ShapeDtypeStruct((1, count), F32)] * sections
        out_specs = [pl.BlockSpec((1, count), whole)] * sections
        scratch = [pltpu.VMEM(best, F32)]
    else:
        out_shape = jax.ShapeDtypeStruct(best, F32)
        out_specs = pl.BlockSpec(best, whole)
    return pl.pallas_call(
        functools.partial(search_kernel, first=before is None, last=last),
        out_shape=out_shape,
        grid=(chunk // tile,),
        in_specs=in_specs,
        out_specs=out_specs,
        scratch_shapes=scratch,
        compiler_params=pltpu.CompilerParams(
            dimension_semantics=("arbitrary",), vmem_limit_bytes=28 << 20
        ),
        cost_estimate=pl.CostEstimate(
            flops=4 * chunk * width * sections * count,
            bytes_accessed=len(points) * width * count * 2 + chunk * width * 4,
            transcendentals=0,
        ),
        name="search",
    )(*args)


def step(points, owner, member, centroids):
    lists, _ = centroids.shape
    count = points.shape[0]
    blocks = lax.axis_size("blk")
    slots = 2 * count // blocks
    both = ("blk", "dim")
    mine = lax.axis_index("blk")
    side = lax.axis_index("dim")
    ids = [(b, d) for b in range(blocks) for d in range(2)]

    def fetch(x, source, odd=False):
        route = []
        for b, d in ids:
            if odd and not b & 2:
                continue
            sb, sd = source(b, d)
            route.append(((sb % blocks) * 2 + sd, b * 2 + d))
        return lax.ppermute(x, both, route)

    near_owner = fetch(owner, lambda b, d: (b ^ 2, d))
    near_member = fetch(member, lambda b, d: (b ^ 2, d))
    near_own = fetch(points, lambda b, d: (b ^ 2, d))
    near_other = fetch(points, lambda b, d: (b ^ 2, 1 - d))

    planes = [[b for b in range(blocks) if (b >> 1) & 1 == z] for z in range(2)]
    owners = blocks // 2
    spot = (mine // 4) * 2 + mine % 2
    lane = ((spot % (LANES // slots)) * slots).astype(I32).reshape(1)
    plane = ((mine // 2) % 2).astype(I32).reshape(1)

    def deliver(owner, member, rows):
        sent = pack(
            lane, plane, owner.reshape(1, count), member.reshape(1, count), rows, owners, slots
        )
        return lax.all_to_all(
            sent, "blk", split_axis=0, concat_axis=0, axis_index_groups=planes, tiled=True
        )

    near_rows = pltpu.with_memory_space_constraint(near_own, pltpu.HBM)
    got = [deliver(owner, member, points), deliver(near_owner, near_member, near_rows)]

    own_0 = turn(points)
    half = count // 2
    other_0 = turn(
        fetch(near_own[:half], lambda b, d: (b ^ 2, 1 - d)),
        fetch(near_other[half:], lambda b, d: (b ^ 2, d)),
    )
    near_own = turn(near_own)
    near_other = turn(near_other)
    far = lambda b, d: (b + 4, d)
    odd = (mine // 2) % 2 == 1
    own_2 = jnp.where(odd, fetch(near_own, far, odd=True), near_own)
    other_2 = jnp.where(odd, fetch(near_other, far, odd=True), near_other)
    even = mine % 2 == 0
    own_1 = fetch(jnp.where(even, own_2, own_0), lambda b, d: (b ^ 1, d))
    other_1 = fetch(jnp.where(even, other_2, other_0), lambda b, d: (b ^ 1, d))
    visitors = [own_0, other_0, own_1, other_1, own_2, other_2]
    squares = jnp.sum(jnp.square(own_0.astype(F32)), axis=0) + jnp.sum(
        jnp.square(other_0.astype(F32)), axis=0
    )

    old = pltpu.with_memory_space_constraint(centroids, pltpu.HBM)
    new_centroids = None
    arrived = []
    done = 0
    for chunk in CHUNKS:
        size = TILE if chunk < 2 * TILE or done % (2 * TILE) else 2 * TILE
        first = (((1 - side) * (lists // 2) + done) // size).astype(I32).reshape(1)
        new_centroids, part = update(first, got, old, new_centroids, chunk, slots, size)
        arrived.append(fetch(part, lambda b, d: (b, 1 - d)))
        done += chunk
    first = (side * (lists // 2) // (2 * TILE)).astype(I32).reshape(1)
    new_centroids, own_half = update(first, got, old, new_centroids, lists // 2, slots, 2 * TILE)

    best = None
    done = 0
    for n, chunk in enumerate(CHUNKS):
        best = search(own_half, done, arrived[n], visitors, best, n == len(CHUNKS) - 1)
        done += chunk
    best = [x.reshape(count) for x in best]
    top = jnp.maximum(best[0], fetch(best[0], lambda b, d: (b, 1 - d)))
    for s in range(1, CYCLE + 1):
        for flip in (0, 1):
            top = jnp.maximum(top, fetch(best[s], lambda b, d: (b - s, d ^ flip)))
    nearest = (squares - 2.0 * top) / D
    return new_centroids, nearest


def solution(mesh):
    in_specs = (P("blk", "dim"), P("blk", None), P("blk"), P("blk", "dim"))
    out_specs = (P("blk", "dim"), P("blk"))
    return jax.shard_map(step, mesh=mesh, in_specs=in_specs, out_specs=out_specs, check_vma=False)
```

```python
import functools

import jax
import jax.numpy as jnp
from jax import lax
from jax.experimental import pallas as pl
from jax.experimental.pallas import tpu as pltpu
from jax.sharding import PartitionSpec as P


D = 1024
CYCLE = 2
LANES = 128
META = 8
TILE = 256
CHUNKS = (512, 1024, 1024, 512, 512, 256, 256)
COLS = 512
PACK_STEPS = 2
BF16 = jnp.bfloat16
F32 = jnp.float32
I32 = jnp.int32


def iota(shape, dim):
    return lax.broadcasted_iota(I32, shape, dim)


def pack_kernel(
    lane_ref, plane_ref, block_ref, member_ref, pts_ref, out_ref, slot_ref, high_ref, low_ref, *, slots
):
    count, width = pts_ref.shape
    tiles = width // LANES
    owners = high_ref.shape[0]
    group = out_ref.shape[0]
    step = pl.program_id(0)

    @pl.when(step == 0)
    def _():
        block = block_ref[...]
        member = member_ref[...]
        here = ((block >> 1) & 1) == plane_ref[0]
        owner = jnp.where(here, (block >> 2) * 2 + (block & 1), -1)
        is_owner = owner == iota((owners, count), 0)
        weights = jnp.where(is_owner, 1.0, 0.0)
        before = jnp.where(iota((LANES, LANES), 0) < iota((LANES, LANES), 1), 1.0, 0.0).astype(BF16)
        earlier = []
        base = jnp.zeros((owners, 1), F32)
        for c in range(0, count, LANES):
            strip = weights[:, c : c + LANES]
            earlier.append(
                base + jnp.dot(strip.astype(BF16), before, preferred_element_type=F32)
            )
            base = base + jnp.sum(strip, axis=1, keepdims=True)
        earlier = jnp.concatenate(earlier, axis=1)
        place = jnp.sum(jnp.where(is_owner, earlier, 0.0), axis=0, keepdims=True).astype(I32)
        slot_ref[...] = jnp.where(here, owner * slots + place, -1)
        lane = jnp.where(iota((LANES, count), 0) == place + lane_ref[0], 1.0, 0.0).astype(BF16)

        def spread(row):
            return lax.dot_general(
                jnp.where(is_owner, row.astype(F32), 0.0).astype(BF16),
                lane,
                (((1,), (1,)), ((), ())),
                preferred_element_type=F32,
            )

        high_ref[...] = spread((member >> 6) + 1)
        low_ref[...] = spread(member & 63)

    row = iota((group, META, LANES), 1)
    mine = pl.ds(pl.multiple_of(step * group, group), group)
    high, low = high_ref[mine, :], low_ref[mine, :]
    out_ref[:, slots * tiles :, :] = jnp.where(
        row == 0, high[:, None, :], jnp.where(row == 1, low[:, None, :], 0.0)
    ).astype(BF16)
    part = TILE // slots
    for p in range(group // part):
        want = iota((TILE, count), 0) + (step * group + p * part) * slots
        pick = jnp.where(want == slot_ref[...], 1.0, 0.0).astype(BF16)
        placed = jnp.dot(pick, pts_ref[...], preferred_element_type=F32).astype(BF16)
        for o in range(part):
            for t in range(tiles):
                out_ref[p * part + o, t * slots : (t + 1) * slots, :] = placed[
                    o * slots : (o + 1) * slots, t * LANES : (t + 1) * LANES
                ]


def pack(lane, plane, block, member, points, owners, slots):
    count, width = points.shape
    rows = slots * (width // LANES) + META
    group = owners // PACK_STEPS
    whole = lambda i: (0, 0)
    return pl.pallas_call(
        functools.partial(pack_kernel, slots=slots),
        out_shape=jax.ShapeDtypeStruct((owners, rows, LANES), BF16),
        grid=(PACK_STEPS,),
        in_specs=[
            pl.BlockSpec(memory_space=pltpu.SMEM),
            pl.BlockSpec(memory_space=pltpu.SMEM),
            pl.BlockSpec((1, count), whole),
            pl.BlockSpec((1, count), whole),
            pl.BlockSpec((count, width), whole),
        ],
        out_specs=pl.BlockSpec((group, rows, LANES), lambda i: (i, 0, 0)),
        scratch_shapes=[
            pltpu.VMEM((1, count), I32),
            pltpu.VMEM((owners, LANES), F32),
            pltpu.VMEM((owners, LANES), F32),
        ],
        compiler_params=pltpu.CompilerParams(
            dimension_semantics=("arbitrary",), vmem_limit_bytes=60 << 20
        ),
        cost_estimate=pl.CostEstimate(
            flops=2 * owners * slots * count * width, bytes_accessed=4 << 20, transcendentals=0
        ),
        name="pack",
    )(lane, plane, block, member, points)


def update_kernel(first_ref, got_a_ref, got_b_ref, old_ref, *refs, owners, slots, chained):
    if chained:
        refs = refs[1:]
    out_ref, part_ref, rows_ref, list_ref = refs
    step = pl.program_id(0)
    size, width = old_ref.shape
    tiles = width // LANES
    share = LANES // slots
    strips = owners // share

    @pl.when(step == 0)
    def _():
        for n, got_ref in enumerate((got_a_ref, got_b_ref)):

            @pl.loop(0, owners, unroll=4)
            def _(o, n=n, got_ref=got_ref):
                at = pl.ds(pl.multiple_of((n * owners + o) * slots, slots), slots)
                for t in range(tiles):
                    rows_ref[at, t * LANES : (t + 1) * LANES] = got_ref[
                        o, t * slots : (t + 1) * slots, :
                    ]

            meta = got_ref[:, slots * tiles :, :].astype(F32)
            row = iota(meta.shape, 1)
            number = jnp.sum(
                jnp.where(row == 0, meta * 64.0, jnp.where(row == 1, meta, 0.0)), axis=1
            )
            number = jnp.sum(number.reshape(strips, share, LANES), axis=1)
            list_ref[n * strips : (n + 1) * strips, :] = number.astype(I32) - 64

    want = iota((size, LANES), 0) + (first_ref[0] + step) * size
    picks = []
    total = jnp.zeros((size, LANES), F32)
    for g in range(2 * strips):
        hit = jnp.where(list_ref[g : g + 1, :] == want, 1.0, 0.0)
        total = total + hit
        picks.append(hit.astype(BF16))
    sums = jnp.dot(jnp.concatenate(picks, axis=1), rows_ref[...], preferred_element_type=F32)
    counts = jnp.sum(total, axis=1, keepdims=True)
    new = ((sums + old_ref[...].astype(F32)) / (counts + 1.0)).astype(BF16)
    out_ref[...] = new
    part_ref[...] = new


def update(first, got, centroids, so_far, count, slots, size=TILE):
    lists, width = centroids.shape
    owners = got[0].shape[0]
    tile = lambda i, first: (first[0] + i, 0)
    chained = so_far is not None
    in_specs = [
        pl.BlockSpec(x.shape, lambda i, first: (0, 0, 0), pipeline_mode=pl.Buffered(1)) for x in got
    ]
    in_specs.append(pl.BlockSpec((size, width), tile))
    args = [first, *got, centroids]
    if chained:
        in_specs.append(pl.BlockSpec(memory_space=pl.ANY))
        args.append(so_far)
    return pl.pallas_call(
        functools.partial(update_kernel, owners=owners, slots=slots, chained=chained),
        out_shape=(
            jax.ShapeDtypeStruct((lists, width), BF16),
            jax.ShapeDtypeStruct((count, width), BF16),
        ),
        grid_spec=pltpu.PrefetchScalarGridSpec(
            num_scalar_prefetch=1,
            grid=(count // size,),
            in_specs=in_specs,
            out_specs=(
                pl.BlockSpec((size, width), tile),
                pl.BlockSpec((size, width), lambda i, first: (i, 0)),
            ),
            scratch_shapes=[
                pltpu.VMEM((2 * owners * slots, width), BF16),
                pltpu.VMEM((2 * owners * slots // LANES, LANES), I32),
            ],
        ),
        input_output_aliases={4: 0} if chained else {},
        compiler_params=pltpu.CompilerParams(
            dimension_semantics=("arbitrary",), vmem_limit_bytes=24 << 20
        ),
        cost_estimate=pl.CostEstimate(
            flops=4 * count * owners * slots * width,
            bytes_accessed=got[0].size * 4 + count * width * 6,
            transcendentals=0,
        ),
        name="update",
    )(*args)


def turn_kernel(*refs):
    out_ref = refs[-1]
    at = 0
    for ref in refs[:-1]:
        rows = ref.shape[0]
        out_ref[:, at : at + rows] = ref[...].T
        at += rows


def turn(*parts):
    width = parts[0].shape[1]
    half = width // 2
    count = sum(x.shape[0] for x in parts)
    return pl.pallas_call(
        turn_kernel,
        out_shape=jax.ShapeDtypeStruct((width, count), BF16),
        grid=(2,),
        in_specs=[pl.BlockSpec((x.shape[0], half), lambda i: (0, i)) for x in parts],
        out_specs=pl.BlockSpec((half, count), lambda i: (i, 0)),
        compiler_params=pltpu.CompilerParams(
            dimension_semantics=("arbitrary",), vmem_limit_bytes=24 << 20
        ),
        cost_estimate=pl.CostEstimate(
            flops=0, bytes_accessed=4 * width * count, transcendentals=0
        ),
        name="turn",
    )(*parts)


def search_kernel(own_ref, other_ref, *refs, first, last):
    sections = CYCLE + 1
    points, refs = refs[: 2 * sections], refs[2 * sections :]
    if not first:
        before_ref, refs = refs[0], refs[1:]
    if last:
        outs, best_ref = refs[:sections], refs[sections]
    else:
        best_ref = refs[0]
    step = pl.program_id(0)
    count = points[0].shape[1]

    @pl.when(step == 0)
    def _():
        best_ref[...] = jnp.full_like(best_ref, -jnp.inf) if first else before_ref[...]

    own, other = own_ref[...], other_ref[...]
    own_f, other_f = own.astype(F32), other.astype(F32)
    half = 0.5 * (
        jnp.sum(own_f * own_f, axis=1, keepdims=True)
        + jnp.sum(other_f * other_f, axis=1, keepdims=True)
    )
    for s in range(sections):
        for c in range(0, count, COLS):
            score = jnp.dot(own, points[2 * s][:, c : c + COLS], preferred_element_type=F32)
            score += jnp.dot(other, points[2 * s + 1][:, c : c + COLS], preferred_element_type=F32)
            score -= half
            top = jnp.max(score.reshape(-1, 8, COLS), axis=0)
            at = slice(s * count + c, s * count + c + COLS)
            best_ref[:, at] = jnp.maximum(best_ref[:, at], top)

    if last:

        @pl.when(step == pl.num_programs(0) - 1)
        def _():
            for s in range(sections):
                outs[s][...] = jnp.max(
                    best_ref[:, s * count : (s + 1) * count], axis=0, keepdims=True
                )


def search(own, offset, other, points, before, last):
    chunk, width = other.shape
    sections = CYCLE + 1
    count = points[0].shape[1]
    tile = TILE if chunk % (4 * TILE) or offset % (2 * TILE) else 2 * TILE
    whole = lambda i: (0, 0)
    in_specs = [
        pl.BlockSpec((tile, width), lambda i: (i + offset // tile, 0)),
        pl.BlockSpec((tile, width), lambda i: (i, 0)),
    ]
    in_specs += [pl.BlockSpec((width, count), whole, pipeline_mode=pl.Buffered(1))] * len(points)
    args = [own, other, *points]
    best = (8, sections * count)
    if before is not None:
        in_specs.append(pl.BlockSpec(best, whole))
        args.append(before)
    scratch = []
    if last:
        out_shape = [jax.ShapeDtypeStruct((1, count), F32)] * sections
        out_specs = [pl.BlockSpec((1, count), whole)] * sections
        scratch = [pltpu.VMEM(best, F32)]
    else:
        out_shape = jax.ShapeDtypeStruct(best, F32)
        out_specs = pl.BlockSpec(best, whole)
    return pl.pallas_call(
        functools.partial(search_kernel, first=before is None, last=last),
        out_shape=out_shape,
        grid=(chunk // tile,),
        in_specs=in_specs,
        out_specs=out_specs,
        scratch_shapes=scratch,
        compiler_params=pltpu.CompilerParams(
            dimension_semantics=("arbitrary",), vmem_limit_bytes=28 << 20
        ),
        cost_estimate=pl.CostEstimate(
            flops=4 * chunk * width * sections * count,
            bytes_accessed=len(points) * width * count * 2 + chunk * width * 4,
            transcendentals=0,
        ),
        name="search",
    )(*args)


def step(points, owner, member, centroids):
    lists, _ = centroids.shape
    count = points.shape[0]
    blocks = lax.axis_size("blk")
    slots = 2 * count // blocks
    both = ("blk", "dim")
    mine = lax.axis_index("blk")
    side = lax.axis_index("dim")
    ids = [(b, d) for b in range(blocks) for d in range(2)]

    def fetch(x, source, odd=False):
        route = []
        for b, d in ids:
            if odd and not b & 2:
                continue
            sb, sd = source(b, d)
            route.append(((sb % blocks) * 2 + sd, b * 2 + d))
        return lax.ppermute(x, both, route)

    near_owner = fetch(owner, lambda b, d: (b ^ 2, d))
    near_member = fetch(member, lambda b, d: (b ^ 2, d))
    near_own = fetch(points, lambda b, d: (b ^ 2, d))
    near_other = fetch(points, lambda b, d: (b ^ 2, 1 - d))

    planes = [[b for b in range(blocks) if (b >> 1) & 1 == z] for z in range(2)]
    owners = blocks // 2
    spot = (mine // 4) * 2 + mine % 2
    lane = ((spot % (LANES // slots)) * slots).astype(I32).reshape(1)
    plane = ((mine // 2) % 2).astype(I32).reshape(1)

    def deliver(owner, member, rows):
        sent = pack(
            lane, plane, owner.reshape(1, count), member.reshape(1, count), rows, owners, slots
        )
        return lax.all_to_all(
            sent, "blk", split_axis=0, concat_axis=0, axis_index_groups=planes, tiled=True
        )

    near_rows = pltpu.with_memory_space_constraint(near_own, pltpu.HBM)
    got = [deliver(owner, member, points), deliver(near_owner, near_member, near_rows)]

    own_0 = turn(points)
    half = count // 2
    other_0 = turn(
        fetch(near_own[:half], lambda b, d: (b ^ 2, 1 - d)),
        fetch(near_other[half:], lambda b, d: (b ^ 2, d)),
    )
    near_own = turn(near_own)
    near_other = turn(near_other)
    far = lambda b, d: (b + 4, d)
    odd = (mine // 2) % 2 == 1
    own_2 = jnp.where(odd, fetch(near_own, far, odd=True), near_own)
    other_2 = jnp.where(odd, fetch(near_other, far, odd=True), near_other)
    even = mine % 2 == 0
    own_1 = fetch(jnp.where(even, own_2, own_0), lambda b, d: (b ^ 1, d))
    other_1 = fetch(jnp.where(even, other_2, other_0), lambda b, d: (b ^ 1, d))
    visitors = [own_0, other_0, own_1, other_1, own_2, other_2]
    squares = jnp.sum(jnp.square(own_0.astype(F32)), axis=0) + jnp.sum(
        jnp.square(other_0.astype(F32)), axis=0
    )

    old = pltpu.with_memory_space_constraint(centroids, pltpu.HBM)
    new_centroids = None
    arrived = []
    done = 0
    for chunk in CHUNKS:
        size = TILE if chunk < 2 * TILE or done % (2 * TILE) else 2 * TILE
        first = (((1 - side) * (lists // 2) + done) // size).astype(I32).reshape(1)
        new_centroids, part = update(first, got, old, new_centroids, chunk, slots, size)
        arrived.append(fetch(part, lambda b, d: (b, 1 - d)))
        done += chunk
    first = (side * (lists // 2) // (2 * TILE)).astype(I32).reshape(1)
    new_centroids, own_half = update(first, got, old, new_centroids, lists // 2, slots, 2 * TILE)

    best = None
    done = 0
    for n, chunk in enumerate(CHUNKS):
        best = search(own_half, done, arrived[n], visitors, best, n == len(CHUNKS) - 1)
        done += chunk
    best = [x.reshape(count) for x in best]
    other_core = fetch(best[1], lambda b, d: (b ^ 1, d))
    here = jnp.where(even, best[0], jnp.maximum(best[0], other_core))
    onward = jnp.where(even, jnp.maximum(best[2], other_core), best[2])
    top = jnp.maximum(here, fetch(here, lambda b, d: (b, 1 - d)))
    for flip in (0, 1):
        top = jnp.maximum(top, fetch(onward, lambda b, d: (b - 2, d ^ flip)))
    nearest = (squares - 2.0 * top) / D
    return new_centroids, nearest


def solution(mesh):
    in_specs = (P("blk", "dim"), P("blk", None), P("blk"), P("blk", "dim"))
    out_specs = (P("blk", "dim"), P("blk"))
    return jax.shard_map(step, mesh=mesh, in_specs=in_specs, out_specs=out_specs, check_vma=False)
```

```python
import functools

import jax
import jax.numpy as jnp
from jax import lax
from jax.experimental import pallas as pl
from jax.experimental.pallas import tpu as pltpu
from jax.sharding import PartitionSpec as P


D = 1024
CYCLE = 2
LANES = 128
META = 8
TILE = 256
CHUNKS = (512, 1024, 1024, 512, 512, 256, 256)
COLS = 512
PACK_STEPS = 1
BF16 = jnp.bfloat16
F32 = jnp.float32
I32 = jnp.int32


def iota(shape, dim):
    return lax.broadcasted_iota(I32, shape, dim)


def pack_kernel(
    lane_ref, plane_ref, block_ref, member_ref, pts_ref, out_ref, slot_ref, high_ref, low_ref, *, slots
):
    count, width = pts_ref.shape
    tiles = width // LANES
    owners = high_ref.shape[0]
    group = out_ref.shape[0]
    step = pl.program_id(0)

    @pl.when(step == 0)
    def _():
        block = block_ref[...]
        member = member_ref[...]
        here = ((block >> 1) & 1) == plane_ref[0]
        owner = jnp.where(here, (block >> 2) * 2 + (block & 1), -1)
        is_owner = owner == iota((owners, count), 0)
        weights = jnp.where(is_owner, 1.0, 0.0)
        before = jnp.where(iota((LANES, LANES), 0) < iota((LANES, LANES), 1), 1.0, 0.0).astype(BF16)
        earlier = []
        base = jnp.zeros((owners, 1), F32)
        for c in range(0, count, LANES):
            strip = weights[:, c : c + LANES]
            earlier.append(
                base + jnp.dot(strip.astype(BF16), before, preferred_element_type=F32)
            )
            base = base + jnp.sum(strip, axis=1, keepdims=True)
        earlier = jnp.concatenate(earlier, axis=1)
        place = jnp.sum(jnp.where(is_owner, earlier, 0.0), axis=0, keepdims=True).astype(I32)
        slot_ref[...] = jnp.where(here, owner * slots + place, -1)
        lane = jnp.where(iota((LANES, count), 0) == place + lane_ref[0], 1.0, 0.0).astype(BF16)

        def spread(row):
            return lax.dot_general(
                jnp.where(is_owner, row.astype(F32), 0.0).astype(BF16),
                lane,
                (((1,), (1,)), ((), ())),
                preferred_element_type=F32,
            )

        high_ref[...] = spread((member >> 6) + 1)
        low_ref[...] = spread(member & 63)

    row = iota((group, META, LANES), 1)
    mine = pl.ds(pl.multiple_of(step * group, group), group)
    high, low = high_ref[mine, :], low_ref[mine, :]
    out_ref[:, slots * tiles :, :] = jnp.where(
        row == 0, high[:, None, :], jnp.where(row == 1, low[:, None, :], 0.0)
    ).astype(BF16)
    part = TILE // slots
    for p in range(group // part):
        want = iota((TILE, count), 0) + (step * group + p * part) * slots
        pick = jnp.where(want == slot_ref[...], 1.0, 0.0).astype(BF16)
        placed = jnp.dot(pick, pts_ref[...], preferred_element_type=F32).astype(BF16)
        for o in range(part):
            for t in range(tiles):
                out_ref[p * part + o, t * slots : (t + 1) * slots, :] = placed[
                    o * slots : (o + 1) * slots, t * LANES : (t + 1) * LANES
                ]


def pack(lane, plane, block, member, points, owners, slots, limit):
    count, width = points.shape
    rows = slots * (width // LANES) + META
    group = owners // PACK_STEPS
    whole = lambda i: (0, 0)
    return pl.pallas_call(
        functools.partial(pack_kernel, slots=slots),
        out_shape=jax.ShapeDtypeStruct((owners, rows, LANES), BF16),
        grid=(PACK_STEPS,),
        in_specs=[
            pl.BlockSpec(memory_space=pltpu.SMEM),
            pl.BlockSpec(memory_space=pltpu.SMEM),
            pl.BlockSpec((1, count), whole),
            pl.BlockSpec((1, count), whole),
            pl.BlockSpec((count, width), whole),
        ],
        out_specs=pl.BlockSpec((group, rows, LANES), lambda i: (i, 0, 0)),
        scratch_shapes=[
            pltpu.VMEM((1, count), I32),
            pltpu.VMEM((owners, LANES), F32),
            pltpu.VMEM((owners, LANES), F32),
        ],
        compiler_params=pltpu.CompilerParams(
            dimension_semantics=("arbitrary",), vmem_limit_bytes=limit
        ),
        cost_estimate=pl.CostEstimate(
            flops=2 * owners * slots * count * width, bytes_accessed=4 << 20, transcendentals=0
        ),
        name="pack",
    )(lane, plane, block, member, points)


def update_kernel(first_ref, got_a_ref, got_b_ref, old_ref, *refs, owners, slots, chained):
    if chained:
        refs = refs[1:]
    out_ref, part_ref, rows_ref, list_ref = refs
    step = pl.program_id(0)
    size, width = old_ref.shape
    tiles = width // LANES
    share = LANES // slots
    strips = owners // share

    @pl.when(step == 0)
    def _():
        for n, got_ref in enumerate((got_a_ref, got_b_ref)):

            @pl.loop(0, owners, unroll=4)
            def _(o, n=n, got_ref=got_ref):
                at = pl.ds(pl.multiple_of((n * owners + o) * slots, slots), slots)
                for t in range(tiles):
                    rows_ref[at, t * LANES : (t + 1) * LANES] = got_ref[
                        o, t * slots : (t + 1) * slots, :
                    ]

            meta = got_ref[:, slots * tiles :, :].astype(F32)
            row = iota(meta.shape, 1)
            number = jnp.sum(
                jnp.where(row == 0, meta * 64.0, jnp.where(row == 1, meta, 0.0)), axis=1
            )
            number = jnp.sum(number.reshape(strips, share, LANES), axis=1)
            list_ref[n * strips : (n + 1) * strips, :] = number.astype(I32) - 64

    want = iota((size, LANES), 0) + (first_ref[0] + step) * size
    picks = []
    total = jnp.zeros((size, LANES), F32)
    for g in range(2 * strips):
        hit = jnp.where(list_ref[g : g + 1, :] == want, 1.0, 0.0)
        total = total + hit
        picks.append(hit.astype(BF16))
    sums = jnp.dot(jnp.concatenate(picks, axis=1), rows_ref[...], preferred_element_type=F32)
    counts = jnp.sum(total, axis=1, keepdims=True)
    new = ((sums + old_ref[...].astype(F32)) / (counts + 1.0)).astype(BF16)
    out_ref[...] = new
    part_ref[...] = new


def update(first, got, centroids, so_far, count, slots, size=TILE):
    lists, width = centroids.shape
    owners = got[0].shape[0]
    tile = lambda i, first: (first[0] + i, 0)
    chained = so_far is not None
    in_specs = [
        pl.BlockSpec(x.shape, lambda i, first: (0, 0, 0), pipeline_mode=pl.Buffered(1)) for x in got
    ]
    in_specs.append(pl.BlockSpec((size, width), tile))
    args = [first, *got, centroids]
    if chained:
        in_specs.append(pl.BlockSpec(memory_space=pl.ANY))
        args.append(so_far)
    return pl.pallas_call(
        functools.partial(update_kernel, owners=owners, slots=slots, chained=chained),
        out_shape=(
            jax.ShapeDtypeStruct((lists, width), BF16),
            jax.ShapeDtypeStruct((count, width), BF16),
        ),
        grid_spec=pltpu.PrefetchScalarGridSpec(
            num_scalar_prefetch=1,
            grid=(count // size,),
            in_specs=in_specs,
            out_specs=(
                pl.BlockSpec((size, width), tile),
                pl.BlockSpec((size, width), lambda i, first: (i, 0)),
            ),
            scratch_shapes=[
                pltpu.VMEM((2 * owners * slots, width), BF16),
                pltpu.VMEM((2 * owners * slots // LANES, LANES), I32),
            ],
        ),
        input_output_aliases={4: 0} if chained else {},
        compiler_params=pltpu.CompilerParams(
            dimension_semantics=("arbitrary",), vmem_limit_bytes=24 << 20
        ),
        cost_estimate=pl.CostEstimate(
            flops=4 * count * owners * slots * width,
            bytes_accessed=got[0].size * 4 + count * width * 6,
            transcendentals=0,
        ),
        name="update",
    )(*args)


def turn_kernel(*refs):
    out_ref = refs[-1]
    at = 0
    for ref in refs[:-1]:
        rows = ref.shape[0]
        out_ref[:, at : at + rows] = ref[...].T
        at += rows


def turn(*parts):
    width = parts[0].shape[1]
    half = width // 2
    count = sum(x.shape[0] for x in parts)
    return pl.pallas_call(
        turn_kernel,
        out_shape=jax.ShapeDtypeStruct((width, count), BF16),
        grid=(2,),
        in_specs=[pl.BlockSpec((x.shape[0], half), lambda i: (0, i)) for x in parts],
        out_specs=pl.BlockSpec((half, count), lambda i: (i, 0)),
        compiler_params=pltpu.CompilerParams(
            dimension_semantics=("arbitrary",), vmem_limit_bytes=24 << 20
        ),
        cost_estimate=pl.CostEstimate(
            flops=0, bytes_accessed=4 * width * count, transcendentals=0
        ),
        name="turn",
    )(*parts)


def search_kernel(own_ref, other_ref, *refs, first, last):
    sections = CYCLE + 1
    points, refs = refs[: 2 * sections], refs[2 * sections :]
    if not first:
        before_ref, refs = refs[0], refs[1:]
    if last:
        outs, best_ref = refs[:sections], refs[sections]
    else:
        best_ref = refs[0]
    step = pl.program_id(0)
    count = points[0].shape[1]

    @pl.when(step == 0)
    def _():
        best_ref[...] = jnp.full_like(best_ref, -jnp.inf) if first else before_ref[...]

    own, other = own_ref[...], other_ref[...]
    own_f, other_f = own.astype(F32), other.astype(F32)
    half = 0.5 * (
        jnp.sum(own_f * own_f, axis=1, keepdims=True)
        + jnp.sum(other_f * other_f, axis=1, keepdims=True)
    )
    for s in range(sections):
        for c in range(0, count, COLS):
            score = jnp.dot(own, points[2 * s][:, c : c + COLS], preferred_element_type=F32)
            score += jnp.dot(other, points[2 * s + 1][:, c : c + COLS], preferred_element_type=F32)
            score -= half
            top = jnp.max(score.reshape(-1, 8, COLS), axis=0)
            at = slice(s * count + c, s * count + c + COLS)
            best_ref[:, at] = jnp.maximum(best_ref[:, at], top)

    if last:

        @pl.when(step == pl.num_programs(0) - 1)
        def _():
            for s in range(sections):
                outs[s][...] = jnp.max(
                    best_ref[:, s * count : (s + 1) * count], axis=0, keepdims=True
                )


def search(own, offset, other, points, before, last):
    chunk, width = other.shape
    sections = CYCLE + 1
    count = points[0].shape[1]
    tile = TILE if chunk % (4 * TILE) or offset % (2 * TILE) else 2 * TILE
    whole = lambda i: (0, 0)
    in_specs = [
        pl.BlockSpec((tile, width), lambda i: (i + offset // tile, 0)),
        pl.BlockSpec((tile, width), lambda i: (i, 0)),
    ]
    in_specs += [pl.BlockSpec((width, count), whole, pipeline_mode=pl.Buffered(1))] * len(points)
    args = [own, other, *points]
    best = (8, sections * count)
    if before is not None:
        in_specs.append(pl.BlockSpec(best, whole))
        args.append(before)
    scratch = []
    if last:
        out_shape = [jax.ShapeDtypeStruct((1, count), F32)] * sections
        out_specs = [pl.BlockSpec((1, count), whole)] * sections
        scratch = [pltpu.VMEM(best, F32)]
    else:
        out_shape = jax.ShapeDtypeStruct(best, F32)
        out_specs = pl.BlockSpec(best, whole)
    return pl.pallas_call(
        functools.partial(search_kernel, first=before is None, last=last),
        out_shape=out_shape,
        grid=(chunk // tile,),
        in_specs=in_specs,
        out_specs=out_specs,
        scratch_shapes=scratch,
        compiler_params=pltpu.CompilerParams(
            dimension_semantics=("arbitrary",), vmem_limit_bytes=28 << 20
        ),
        cost_estimate=pl.CostEstimate(
            flops=4 * chunk * width * sections * count,
            bytes_accessed=len(points) * width * count * 2 + chunk * width * 4,
            transcendentals=0,
        ),
        name="search",
    )(*args)


def step(points, owner, member, centroids):
    lists, _ = centroids.shape
    count = points.shape[0]
    blocks = lax.axis_size("blk")
    slots = 2 * count // blocks
    both = ("blk", "dim")
    mine = lax.axis_index("blk")
    side = lax.axis_index("dim")
    ids = [(b, d) for b in range(blocks) for d in range(2)]

    def fetch(x, source, odd=False):
        route = []
        for b, d in ids:
            if odd and not b & 2:
                continue
            sb, sd = source(b, d)
            route.append(((sb % blocks) * 2 + sd, b * 2 + d))
        return lax.ppermute(x, both, route)

    near_owner = fetch(owner, lambda b, d: (b ^ 2, d))
    near_member = fetch(member, lambda b, d: (b ^ 2, d))
    near_own = fetch(points, lambda b, d: (b ^ 2, d))
    near_other = fetch(points, lambda b, d: (b ^ 2, 1 - d))

    planes = [[b for b in range(blocks) if (b >> 1) & 1 == z] for z in range(2)]
    owners = blocks // 2
    spot = (mine // 4) * 2 + mine % 2
    lane = ((spot % (LANES // slots)) * slots).astype(I32).reshape(1)
    plane = ((mine // 2) % 2).astype(I32).reshape(1)

    def deliver(owner, member, rows, limit):
        sent = pack(
            lane, plane, owner.reshape(1, count), member.reshape(1, count), rows, owners, slots, limit
        )
        return lax.all_to_all(
            sent, "blk", split_axis=0, concat_axis=0, axis_index_groups=planes, tiled=True
        )

    got = [
        deliver(owner, member, points, 60 << 20),
        deliver(near_owner, near_member, near_own, 20 << 20),
    ]

    own_0 = turn(points)
    half = count // 2
    other_0 = turn(
        fetch(near_own[:half], lambda b, d: (b ^ 2, 1 - d)),
        fetch(near_other[half:], lambda b, d: (b ^ 2, d)),
    )
    near_own = turn(near_own)
    near_other = turn(near_other)
    far = lambda b, d: (b + 4, d)
    odd = (mine // 2) % 2 == 1
    own_2 = jnp.where(odd, fetch(near_own, far, odd=True), near_own)
    other_2 = jnp.where(odd, fetch(near_other, far, odd=True), near_other)
    even = mine % 2 == 0
    own_1 = fetch(jnp.where(even, own_2, own_0), lambda b, d: (b ^ 1, d))
    other_1 = fetch(jnp.where(even, other_2, other_0), lambda b, d: (b ^ 1, d))
    visitors = [own_0, other_0, own_1, other_1, own_2, other_2]
    squares = jnp.sum(jnp.square(own_0.astype(F32)), axis=0) + jnp.sum(
        jnp.square(other_0.astype(F32)), axis=0
    )

    old = pltpu.with_memory_space_constraint(centroids, pltpu.HBM)
    new_centroids = None
    arrived = []
    done = 0
    for chunk in CHUNKS:
        size = TILE if chunk < 2 * TILE or done % (2 * TILE) else 2 * TILE
        first = (((1 - side) * (lists // 2) + done) // size).astype(I32).reshape(1)
        new_centroids, part = update(first, got, old, new_centroids, chunk, slots, size)
        arrived.append(fetch(part, lambda b, d: (b, 1 - d)))
        done += chunk
    first = (side * (lists // 2) // (2 * TILE)).astype(I32).reshape(1)
    new_centroids, own_half = update(first, got, old, new_centroids, lists // 2, slots, 2 * TILE)

    best = None
    done = 0
    for n, chunk in enumerate(CHUNKS):
        best = search(own_half, done, arrived[n], visitors, best, n == len(CHUNKS) - 1)
        done += chunk
    best = [x.reshape(count) for x in best]
    other_core = fetch(best[1], lambda b, d: (b ^ 1, d))
    here = jnp.where(even, best[0], jnp.maximum(best[0], other_core))
    onward = jnp.where(even, jnp.maximum(best[2], other_core), best[2])
    top = jnp.maximum(here, fetch(here, lambda b, d: (b, 1 - d)))
    for flip in (0, 1):
        top = jnp.maximum(top, fetch(onward, lambda b, d: (b - 2, d ^ flip)))
    nearest = (squares - 2.0 * top) / D
    return new_centroids, nearest


def solution(mesh):
    in_specs = (P("blk", "dim"), P("blk", None), P("blk"), P("blk", "dim"))
    out_specs = (P("blk", "dim"), P("blk"))
    return jax.shard_map(step, mesh=mesh, in_specs=in_specs, out_specs=out_specs, check_vma=False)
```
